32 devices in a mesh: tok: 8 (over z, x), layer: 4 (over y, core).
Axes of the slice: x: 2, y: 2, z: 4, core: 2. Of those that a mesh axis runs over, the one named last changes fastest.
Arguments:
- activations: bfloat16 [4, 6144, 2048], P('layer', 'tok'), may hold values from -6 to 6
- gradients: bfloat16 [4, 6144, 4096], P('layer', 'tok'), may hold values from -6 to 6
- query_out: float32 [4, 128, 4096], P('layer', 'tok'), may hold values from -0.0234375 to 0.0234375
- query_in: float32 [4, 128, 2048], P('layer', 'tok'), may hold values from -0.03125 to 0.03125
- out_inverse: float32 [4, 16, 256, 256], P('layer', None, 'tok'), as said below
- in_inverse: float32 [4, 8, 256, 256], P('layer', None, 'tok'), as said below
- column_order: int32 [128], replicated, may hold values from 0 to 127, each once
Outputs:
- scores: float32 [6144, 16], P('tok', 'layer')
The draws below stay inside these ranges and needn't reach their ends.
Inputs may be any that keep to these rules, and one draw needn't show every extreme that they name: `column_order`: each value appears exactly once. `out_inverse`: every block is symmetric. `in_inverse`: every block is symmetric.
All inputs are finite; a program needn't handle non-finite values.
Results may differ from the reference program's by a relative error of at most 0.0041.
Values may be sent and summed in bfloat16 or wider, within the bound.
No kernel may reach another device: no remote copies, remote signals or barrier semaphores. Data moves between devices by JAX's collectives and lax.ppermute only.
A program may use at most 64 MiB of HBM per device.

```python
import jax
import jax.numpy as jnp
from jax import lax

DM = 2048
DQ = 4096
BLOCK = 256
QUERIES = 16
RANK = 8
QR = 128
LAYERS = 4
TOKENS = 6144


def symmetric_blocks(key, count):
    first, second = jax.random.split(key, 2)
    shape = (LAYERS, count, BLOCK, BLOCK)
    noise = jax.random.normal(first, shape, jnp.float32)
    spread = (noise + jnp.swapaxes(noise, 2, 3)) / (2.0 * jnp.sqrt(jnp.float32(BLOCK)))
    diagonal = jax.random.uniform(second, (LAYERS, count, BLOCK), jnp.float32, 1.0, 3.0)
    matrix = spread + jnp.eye(BLOCK, dtype=jnp.float32)[None, None] * diagonal[:, :, :, None]
    return matrix


def draw_out_inverse(key, part):
    return symmetric_blocks(jax.random.fold_in(key, 11), DQ // BLOCK)


def draw_in_inverse(key, part):
    return symmetric_blocks(jax.random.fold_in(key, 23), DM // BLOCK)


def block_levels(rng, shape, cuts, smallest, top_value):
    loudness = 1.0
    for axis_at, blocks in cuts:
        draws = jax.random.uniform(jax.random.fold_in(jax.random.fold_in(rng, 6), axis_at), (blocks,), jnp.float32, smallest / len(cuts), top_value / len(cuts))
        loudness = loudness * jnp.repeat(jnp.exp(draws), shape[axis_at] // blocks).reshape((-1,) + (1,) * (len(shape) - 1 - axis_at))
    return loudness


def scatter_about(stream_key, dims, scale, bound, cuts=(), kind=jnp.bfloat16):
    array = jax.random.normal(stream_key, dims, jnp.float32) * scale
    if len(cuts) > 0:
        array = block_levels(stream_key, dims, cuts, -0.22, 0.18) * array
    return jnp.clip(array, min=-bound, max=bound).astype(kind)


def setup_inputs(seed: int = 0) -> dict:
    key_of = jax.random.split(jax.random.key(seed), 8)
    return {
        "activations": scatter_about(key_of[0], (LAYERS, TOKENS, DM), 1.0, 6.0, ((0, 4), (1, 8))),
        "gradients": scatter_about(key_of[1], (LAYERS, TOKENS, DQ), 1.0, 6.0, ((0, 4), (1, 8))),
        "query_out": scatter_about(key_of[2], (LAYERS, QR, DQ), (16 * DQ) ** -0.5, 0.0234375, ((0, 4), (1, 8)), jnp.float32),
        "query_in": scatter_about(key_of[3], (LAYERS, QR, DM), (16 * DM) ** -0.5, 0.03125, ((0, 4), (1, 8)), jnp.float32),
        "out_inverse": draw_out_inverse(jax.random.fold_in(key_of[7], 71), 0),
        "in_inverse": draw_in_inverse(jax.random.fold_in(key_of[7], 71), 0),
        "column_order": jax.random.permutation(key_of[6], QR).astype(jnp.int32),
    }


def precondition(factors, inverse):
    count = factors.shape[0]
    blocks = inverse.shape[0]
    shaped = factors.reshape(count, blocks, inverse.shape[1])
    result = jnp.einsum("bij,cbj->cbi", inverse, shaped, precision=lax.Precision.HIGHEST)
    return result.reshape(count, -1).astype(jnp.bfloat16)


def reference(activations, gradients, query_out, query_in, out_inverse, in_inverse, column_order):
    owners = column_order // RANK
    onehot = (owners[:, None] == jnp.arange(QUERIES, dtype=jnp.int32)[None, :]).astype(jnp.float32)
    summed = jnp.zeros((TOKENS, QUERIES), jnp.float32)
    for layer_index in range(LAYERS):
        ready_out = precondition(query_out[layer_index], out_inverse[layer_index])
        ready_in = precondition(query_in[layer_index], in_inverse[layer_index])
        proj_out = jnp.dot(gradients[layer_index], ready_out.T, preferred_element_type=jnp.float32)
        proj_in = jnp.dot(activations[layer_index], ready_in.T, preferred_element_type=jnp.float32)
        summed = summed + jnp.dot(proj_out * proj_in, onehot, precision=lax.Precision.HIGHEST)
    return summed
```

```python
import functools

import jax
import jax.numpy as jnp
from jax import lax
from jax.experimental import pallas as pl
from jax.experimental.pallas import tpu as pltpu
from jax.sharding import PartitionSpec as P

QUERIES = 16
RANK = 8
SCALE = 2.0**20


def ring_order(n):
    if n % 2:
        return list(range(n))
    return list(range(0, n, 2)) + list(range(n - 1, 0, -2))


def ring_owner(me, shift, n):
    if n % 2:
        return lax.rem(me - shift + n, n)
    place = jnp.where(me % 2 == 0, me // 2, n - 1 - me // 2)
    source = lax.rem(place - shift + n, n)
    return jnp.where(source < n // 2, 2 * source, 2 * (n - 1 - source) + 1)


def ring_gather(shard, axis, n, split):
    order = ring_order(n)
    ahead = [(order[i], order[(i + 1) % n]) for i in range(n)]
    behind = [(order[i], order[(i - 1) % n]) for i in range(n)]
    found = [(0, 0, shard)]
    up, down = shard, shard
    for step in range(1, (n - 1) // 2 + 1):
        up = lax.ppermute(up, axis, ahead)
        down = lax.ppermute(down, axis, behind)
        found += [(step, 0, up), (-step, 0, down)]
    if n % 2 == 0 and n > 1:
        half = shard.shape[split] // 2
        first = lax.slice_in_dim(up, 0, half, axis=split)
        second = lax.slice_in_dim(down, half, shard.shape[split], axis=split)
        found += [
            (n // 2, 0, lax.ppermute(first, axis, ahead)),
            (n // 2, half, lax.ppermute(second, axis, behind)),
        ]
    return found


def split_two(value):
    high = value.astype(jnp.bfloat16)
    return high, (value - high.astype(jnp.float32)).astype(jnp.bfloat16)


NT = (((1,), (1,)), ((), ()))


def precondition_body(n, places, me, out_inverse, in_inverse, *refs):
    shards, ready, whole = refs[: len(places)], refs[len(places)], refs[len(places) + 1]
    for (shift, start), shard in zip(places, shards):
        whole[ring_owner(me[0], shift, n), :, start : start + shard.shape[1]] = shard[...]
    terms, block = whole.shape[0] * whole.shape[1], out_inverse.shape[2]
    piece, count = out_inverse.shape[1], out_inverse.shape[0]
    for b in range(ready.shape[0]):
        inverse = out_inverse[b] if b < count else in_inverse[b - count]
        columns = whole[:, :, b * block : (b + 1) * block].reshape(terms, block)
        stacked = jnp.concatenate(split_two(inverse), axis=0)
        query_high, query_low = split_two(columns)
        by_high = lax.dot_general(stacked, query_high, NT, preferred_element_type=jnp.float32)
        by_low = lax.dot_general(stacked, query_low, NT, preferred_element_type=jnp.float32)
        result = by_high[:piece] + (by_high[piece:] + by_low[:piece] + by_low[piece:])
        ready[b] = result.astype(jnp.bfloat16)


def precondition(me, n, found, out_inverse, in_inverse):
    places = [(shift, start) for shift, start, _ in found]
    shards = [part for _, _, part in found]
    rows, width = shards[0].shape
    blocks = out_inverse.shape[0] + in_inverse.shape[0]
    vmem = pl.BlockSpec(memory_space=pltpu.VMEM)
    return pl.pallas_call(
        functools.partial(precondition_body, n, places),
        out_shape=jax.ShapeDtypeStruct((blocks, out_inverse.shape[1], n * rows), jnp.bfloat16),
        in_specs=[pl.BlockSpec(memory_space=pltpu.SMEM)] + [vmem] * (2 + len(shards)),
        out_specs=vmem,
        scratch_shapes=[pltpu.VMEM((n, rows, width), jnp.float32)],
        name="precondition",
    )(me, out_inverse, in_inverse, *shards)


def project_body(n, places, me, owners, gradients, activations, *refs):
    shards, scores, full = refs[: len(places)], refs[len(places)], refs[len(places) + 1]

    @pl.when(pl.program_id(0) == 0)
    def _():
        for (shift, start), shard in zip(places, shards):
            blocks, piece, _ = shard.shape
            owner = ring_owner(me[0], shift, n)
            for b in range(blocks):
                base = pl.multiple_of((start + b) * n * piece + owner * piece, piece)
                full[pl.ds(base, piece), :] = shard[b]

    dq = gradients.shape[1]
    proj_out = jnp.dot(gradients[...], full[:dq], preferred_element_type=jnp.float32)
    proj_in = jnp.dot(activations[...], full[dq:], preferred_element_type=jnp.float32)
    queries = lax.broadcasted_iota(jnp.int32, (QUERIES, owners.shape[1]), 0)
    onehot = (queries == owners[...]).astype(jnp.float32)
    scores[...] = lax.dot_general(
        onehot, proj_out * proj_in, NT, precision=lax.Precision.HIGHEST, preferred_element_type=jnp.float32
    )


def project(me, n, found, gradients, activations, owners):
    places = [(shift, start) for shift, start, _ in found]
    shards = [part for _, _, part in found]
    tokens, dq = gradients.shape
    dm = activations.shape[1]
    terms = owners.shape[1]
    tile = 256 if tokens % 256 == 0 else tokens
    whole = lambda part: pl.BlockSpec(part.shape, lambda i: (0,) * part.ndim)
    return pl.pallas_call(
        functools.partial(project_body, n, places),
        grid=(tokens // tile,),
        out_shape=jax.ShapeDtypeStruct((QUERIES, tokens), jnp.float32),
        in_specs=[
            pl.BlockSpec(memory_space=pltpu.SMEM),
            whole(owners),
            pl.BlockSpec((tile, dq), lambda i: (i, 0)),
            pl.BlockSpec((tile, dm), lambda i: (i, 0)),
        ]
        + [whole(part) for part in shards],
        out_specs=pl.BlockSpec((QUERIES, tile), lambda i: (0, i)),
        scratch_shapes=[pltpu.VMEM((dq + dm, terms), jnp.bfloat16)],
        name="project",
    )(me, owners, gradients, activations, *shards)


def assemble(me, n, found, split):
    shape = found[0][2].shape
    whole = jnp.zeros((n,) + shape, found[0][2].dtype)
    for shift, start, part in found:
        at = [ring_owner(me, shift, n)] + [0] * len(shape)
        at[1 + split] = start
        whole = lax.dynamic_update_slice(whole, part[None], at)
    return whole


def per_device(n_tok, n_layer, activations, gradients, query_out, query_in, out_inverse, in_inverse, column_order):
    activations, gradients = activations[0], gradients[0]
    out_inverse, in_inverse = out_inverse[0], in_inverse[0]
    rows_here = query_out.shape[1]
    piece, block = out_inverse.shape[1:]
    terms = rows_here * n_tok
    kernels = rows_here % 8 == 0 and piece % 16 == 0
    me = lax.axis_index("tok").astype(jnp.int32)

    query = jnp.concatenate([query_out[0], query_in[0]], axis=1)
    packed = (query * SCALE).astype(jnp.float16)
    found = [
        (shift, start, part.astype(jnp.float32) * (1.0 / SCALE))
        for shift, start, part in ring_gather(packed, "tok", n_tok, 1)
    ]
    if kernels:
        ready = precondition(me[None], n_tok, found, out_inverse, in_inverse)
    else:
        inverse = jnp.concatenate([out_inverse, in_inverse], axis=0)
        whole = assemble(me, n_tok, found, 1).reshape(terms, -1, block)
        ready = jnp.einsum("bij,cbj->bic", inverse, whole, precision=lax.Precision.HIGHEST).astype(jnp.bfloat16)

    owners = column_order // RANK
    found = ring_gather(ready, "tok", n_tok, 0)
    if kernels:
        local = project(me[None], n_tok, found, gradients, activations, owners[None])
    else:
        full = jnp.swapaxes(assemble(me, n_tok, found, 0), 0, 1).reshape(-1, terms)
        dq = gradients.shape[1]
        proj_out = jnp.dot(gradients, full[:dq], preferred_element_type=jnp.float32)
        proj_in = jnp.dot(activations, full[dq:], preferred_element_type=jnp.float32)
        onehot = (jnp.arange(QUERIES, dtype=jnp.int32)[:, None] == owners[None, :]).astype(jnp.float32)
        local = jnp.einsum("qc,tc->qt", onehot, proj_out * proj_in, precision=lax.Precision.HIGHEST)

    local = local.reshape(n_layer, QUERIES // n_layer, local.shape[1])
    layer = lax.axis_index("layer")
    total = lax.dynamic_index_in_dim(local, layer, 0, keepdims=False)
    for step in range(1, n_layer):
        send = lax.dynamic_index_in_dim(local, lax.rem(layer + step, n_layer), 0, keepdims=False)
        pairs = [(i, (i + step) % n_layer) for i in range(n_layer)]
        total = total + lax.ppermute(send, "layer", pairs)
    return total.T


def solution(mesh):
    n_tok, n_layer = mesh.shape["tok"], mesh.shape["layer"]
    in_specs = (
        P("layer", "tok", None),
        P("layer", "tok", None),
        P("layer", "tok", None),
        P("layer", "tok", None),
        P("layer", None, "tok", None),
        P("layer", None, "tok", None),
        P(),
    )
    out_specs = P("tok", "layer")

    def body(*args):
        return per_device(n_tok, n_layer, *args)

    return jax.shard_map(body, mesh=mesh, in_specs=in_specs, out_specs=out_specs, check_vma=False)
```

```python
import functools

import jax
import jax.numpy as jnp
from jax import lax
from jax.experimental import pallas as pl
from jax.experimental.pallas import tpu as pltpu
from jax.sharding import PartitionSpec as P

QUERIES = 16
RANK = 8
SCALE = 2.0**20


def ring_order(n):
    if n % 2:
        return list(range(n))
    return list(range(0, n, 2)) + list(range(n - 1, 0, -2))


def ring_owner(me, shift, n):
    if n % 2:
        return lax.rem(me - shift + n, n)
    place = jnp.where(me % 2 == 0, me // 2, n - 1 - me // 2)
    source = lax.rem(place - shift + n, n)
    return jnp.where(source < n // 2, 2 * source, 2 * (n - 1 - source) + 1)


def ring_gather(shard, axis, n, split):
    order = ring_order(n)
    ahead = [(order[i], order[(i + 1) % n]) for i in range(n)]
    behind = [(order[i], order[(i - 1) % n]) for i in range(n)]
    found = [(0, 0, shard)]
    up, down = shard, shard
    for step in range(1, (n - 1) // 2 + 1):
        up = lax.ppermute(up, axis, ahead)
        down = lax.ppermute(down, axis, behind)
        found += [(step, 0, up), (-step, 0, down)]
    if n % 2 == 0 and n > 1:
        half = shard.shape[split] // 2
        first = lax.slice_in_dim(up, 0, half, axis=split)
        second = lax.slice_in_dim(down, half, shard.shape[split], axis=split)
        found += [
            (n // 2, 0, lax.ppermute(first, axis, ahead)),
            (n // 2, half, lax.ppermute(second, axis, behind)),
        ]
    return found


def split_two(value):
    high = value.astype(jnp.bfloat16)
    return high, (value - high.astype(jnp.float32)).astype(jnp.bfloat16)


NT = (((1,), (1,)), ((), ()))
VMEM = pl.BlockSpec(memory_space=pltpu.VMEM)
SMEM = pl.BlockSpec(memory_space=pltpu.SMEM)
PARAMS = pltpu.CompilerParams(vmem_limit_bytes=12 * 2**20)


def precondition_body(n, places, me, inverse, *refs):
    shards, ready, whole = refs[: len(places)], refs[len(places)], refs[len(places) + 1]
    for (shift, start), shard in zip(places, shards):
        whole[ring_owner(me[0], shift, n), :, start : start + shard.shape[1]] = shard[...]
    terms = whole.shape[0] * whole.shape[1]
    blocks, both, block = inverse.shape
    piece = both // 2
    for b in range(blocks):
        columns = whole[:, :, b * block : (b + 1) * block].reshape(terms, block)
        queries = jnp.concatenate(split_two(columns), axis=0)
        parts = lax.dot_general(queries, inverse[b], NT, preferred_element_type=jnp.float32)
        parts = parts[:terms] + parts[terms:]
        ready[b] = (parts[:, :piece] + parts[:, piece:]).T.astype(jnp.bfloat16)


def precondition(me, n, found, inverse):
    rows, width = found[0][2].shape
    blocks, piece, block = inverse.shape
    stacked = jnp.concatenate(split_two(inverse), axis=1)
    return pl.pallas_call(
        functools.partial(precondition_body, n, [item[:2] for item in found]),
        out_shape=jax.ShapeDtypeStruct((blocks, piece, n * rows), jnp.bfloat16),
        in_specs=[SMEM] + [VMEM] * (1 + len(found)),
        out_specs=VMEM,
        scratch_shapes=[pltpu.VMEM((n, rows, width), jnp.float32)],
        compiler_params=PARAMS,
        name="precondition",
    )(me, stacked, *[item[2] for item in found])


def assemble(me, n, found, axis, split):
    shape = list(found[0][2].shape)
    whole = jnp.zeros(shape[:axis] + [n] + shape[axis:], found[0][2].dtype)
    for shift, start, part in found:
        at = [0] * len(shape)
        at[split] = start
        at.insert(axis, ring_owner(me, shift, n))
        whole = lax.dynamic_update_slice(whole, jnp.expand_dims(part, axis), at)
    return whole


def per_device(n_tok, n_layer, activations, gradients, query_out, query_in, out_inverse, in_inverse, column_order):
    activations, gradients = activations[0], gradients[0]
    out_inverse, in_inverse = out_inverse[0], in_inverse[0]
    rows_here = query_out.shape[1]
    piece, block = out_inverse.shape[1:]
    terms = rows_here * n_tok
    dq = gradients.shape[1]
    me = lax.axis_index("tok").astype(jnp.int32)
    layer = lax.axis_index("layer").astype(jnp.int32)

    query = jnp.concatenate([query_out[0], query_in[0]], axis=1)
    packed = (query * SCALE).astype(jnp.float16)
    gathered = ring_gather(packed, "tok", n_tok, 1)
    found = [(shift, start, part.astype(jnp.float32) * (1.0 / SCALE)) for shift, start, part in gathered]
    if rows_here % 8 == 0 and piece % 16 == 0:
        gate = gathered[max(0, len(gathered) - 4)][2]
        out_inverse, in_inverse, _ = lax.optimization_barrier((out_inverse, in_inverse, gate))
        inverse = jnp.concatenate([out_inverse, in_inverse], axis=0)
        ready = precondition(me[None], n_tok, found, inverse)
    else:
        inverse = jnp.concatenate([out_inverse, in_inverse], axis=0)
        whole = assemble(me, n_tok, found, 0, 1).reshape(terms, -1, block)
        ready = jnp.einsum("bij,cbj->bic", inverse, whole, precision=lax.Precision.HIGHEST).astype(jnp.bfloat16)

    full = assemble(me, n_tok, ring_gather(ready, "tok", n_tok, 0), 1, 0).reshape(-1, terms)
    proj_out = jnp.dot(gradients, full[:dq], preferred_element_type=jnp.float32)
    proj_in = jnp.dot(activations, full[dq:], preferred_element_type=jnp.float32)
    owners = column_order // RANK
    onehot = (jnp.arange(QUERIES, dtype=jnp.int32)[:, None] == owners[None, :]).astype(jnp.float32)
    local = jnp.einsum("qc,tc->qt", onehot, proj_out * proj_in, precision=lax.Precision.HIGHEST)
    local = local.reshape(n_layer, QUERIES // n_layer, local.shape[1])

    total = lax.dynamic_index_in_dim(local, layer, 0, keepdims=False)
    for step in range(1, n_layer):
        send = lax.dynamic_index_in_dim(local, lax.rem(layer + step, n_layer), 0, keepdims=False)
        pairs = [(i, (i + step) % n_layer) for i in range(n_layer)]
        total = total + lax.ppermute(send, "layer", pairs)
    return total.T


def solution(mesh):
    n_tok, n_layer = mesh.shape["tok"], mesh.shape["layer"]
    in_specs = (
        P("layer", "tok", None),
        P("layer", "tok", None),
        P("layer", "tok", None),
        P("layer", "tok", None),
        P("layer", None, "tok", None),
        P("layer", None, "tok", None),
        P(),
    )
    out_specs = P("tok", "layer")

    def body(*args):
        return per_device(n_tok, n_layer, *args)

    return jax.shard_map(body, mesh=mesh, in_specs=in_specs, out_specs=out_specs, check_vma=False)
```

```python
import functools

import jax
import jax.numpy as jnp
from jax import lax
from jax.experimental import pallas as pl
from jax.experimental.pallas import tpu as pltpu
from jax.sharding import PartitionSpec as P

QUERIES = 16
RANK = 8
SCALE = 2.0**20


def ring_order(n):
    if n % 2:
        return list(range(n))
    return list(range(0, n, 2)) + list(range(n - 1, 0, -2))


def ring_owner(me, shift, n):
    if n % 2:
        return lax.rem(me - shift + n, n)
    place = jnp.where(me % 2 == 0, me // 2, n - 1 - me // 2)
    source = lax.rem(place - shift + n, n)
    return jnp.where(source < n // 2, 2 * source, 2 * (n - 1 - source) + 1)


def ring_gather(shard, axis, n, split):
    order = ring_order(n)
    ahead = [(order[i], order[(i + 1) % n]) for i in range(n)]
    behind = [(order[i], order[(i - 1) % n]) for i in range(n)]
    found = [(0, 0, shard)]
    up, down = shard, shard
    for step in range(1, (n - 1) // 2 + 1):
        up = lax.ppermute(up, axis, ahead)
        down = lax.ppermute(down, axis, behind)
        found += [(step, 0, up), (-step, 0, down)]
    if n % 2 == 0 and n > 1:
        half = shard.shape[split] // 2
        first = lax.slice_in_dim(up, 0, half, axis=split)
        second = lax.slice_in_dim(down, half, shard.shape[split], axis=split)
        found += [
            (n // 2, 0, lax.ppermute(first, axis, ahead)),
            (n // 2, half, lax.ppermute(second, axis, behind)),
        ]
    return found


def split_two(value):
    high = value.astype(jnp.bfloat16)
    return high, (value - high.astype(jnp.float32)).astype(jnp.bfloat16)


NT = (((1,), (1,)), ((), ()))
VMEM = pl.BlockSpec(memory_space=pltpu.VMEM)
SMEM = pl.BlockSpec(memory_space=pltpu.SMEM)
PARAMS = pltpu.CompilerParams(vmem_limit_bytes=12 * 2**20)


def precondition_body(n, places, me, inverse, *refs):
    shards, ready, whole = refs[: len(places)], refs[len(places)], refs[len(places) + 1]
    for (shift, start), shard in zip(places, shards):
        whole[ring_owner(me[0], shift, n), :, start : start + shard.shape[1]] = shard[...]
    terms = whole.shape[0] * whole.shape[1]
    blocks, both, block = inverse.shape
    piece = both // 2
    for b in range(blocks):
        columns = whole[:, :, b * block : (b + 1) * block].reshape(terms, block)
        queries = jnp.concatenate(split_two(columns), axis=0)
        parts = lax.dot_general(queries, inverse[b], NT, preferred_element_type=jnp.float32)
        parts = parts[:terms] + parts[terms:]
        ready[b] = (parts[:, :piece] + parts[:, piece:]).T.astype(jnp.bfloat16)


def precondition(me, n, found, inverse):
    rows, width = found[0][2].shape
    blocks, piece, block = inverse.shape
    high = lax.reduce_precision(inverse, exponent_bits=8, mantissa_bits=7)
    stacked = jnp.concatenate([high, inverse - high], axis=1).astype(jnp.bfloat16)
    return pl.pallas_call(
        functools.partial(precondition_body, n, [item[:2] for item in found]),
        out_shape=jax.ShapeDtypeStruct((blocks, piece, n * rows), jnp.bfloat16),
        in_specs=[SMEM] + [VMEM] * (1 + len(found)),
        out_specs=VMEM,
        scratch_shapes=[pltpu.VMEM((n, rows, width), jnp.float32)],
        compiler_params=PARAMS,
        name="precondition",
    )(me, stacked, *[item[2] for item in found])


def assemble(me, n, found, axis, split):
    shape = list(found[0][2].shape)
    whole = jnp.zeros(shape[:axis] + [n] + shape[axis:], found[0][2].dtype)
    for shift, start, part in found:
        at = [0] * len(shape)
        at[split] = start
        at.insert(axis, ring_owner(me, shift, n))
        whole = lax.dynamic_update_slice(whole, jnp.expand_dims(part, axis), at)
    return whole


def per_device(n_tok, n_layer, activations, gradients, query_out, query_in, out_inverse, in_inverse, column_order):
    activations, gradients = activations[0], gradients[0]
    out_inverse, in_inverse = out_inverse[0], in_inverse[0]
    rows_here = query_out.shape[1]
    piece, block = out_inverse.shape[1:]
    terms = rows_here * n_tok
    dq = gradients.shape[1]
    me = lax.axis_index("tok").astype(jnp.int32)
    layer = lax.axis_index("layer").astype(jnp.int32)

    query = jnp.concatenate([query_out[0], query_in[0]], axis=1)
    packed = (query * SCALE).astype(jnp.float16)
    gathered = ring_gather(packed, "tok", n_tok, 1)
    found = [(shift, start, part.astype(jnp.float32) * (1.0 / SCALE)) for shift, start, part in gathered]
    if rows_here % 8 == 0 and piece % 16 == 0:
        gate = gathered[max(0, len(gathered) - 4)][2]
        out_inverse, in_inverse, _ = lax.optimization_barrier((out_inverse, in_inverse, gate))
        inverse = jnp.concatenate([out_inverse, in_inverse], axis=0)
        ready = precondition(me[None], n_tok, found, inverse)
    else:
        inverse = jnp.concatenate([out_inverse, in_inverse], axis=0)
        whole = assemble(me, n_tok, found, 0, 1).reshape(terms, -1, block)
        ready = jnp.einsum("bij,cbj->bic", inverse, whole, precision=lax.Precision.HIGHEST).astype(jnp.bfloat16)

    full = assemble(me, n_tok, ring_gather(ready, "tok", n_tok, 0), 1, 0).reshape(-1, terms)
    proj_out = jnp.dot(gradients, full[:dq], preferred_element_type=jnp.float32)
    proj_in = jnp.dot(activations, full[dq:], preferred_element_type=jnp.float32)
    owners = column_order // RANK
    onehot = (jnp.arange(QUERIES, dtype=jnp.int32)[:, None] == owners[None, :]).astype(jnp.float32)
    local = jnp.einsum("qc,tc->qt", onehot, proj_out * proj_in, precision=lax.Precision.HIGHEST)
    local = local.reshape(n_layer, QUERIES // n_layer, local.shape[1])

    total = lax.dynamic_index_in_dim(local, layer, 0, keepdims=False)
    for step in range(1, n_layer):
        send = lax.dynamic_index_in_dim(local, lax.rem(layer + step, n_layer), 0, keepdims=False)
        pairs = [(i, (i + step) % n_layer) for i in range(n_layer)]
        total = total + lax.ppermute(send, "layer", pairs)
    return total.T


def solution(mesh):
    n_tok, n_layer = mesh.shape["tok"], mesh.shape["layer"]
    in_specs = (
        P("layer", "tok", None),
        P("layer", "tok", None),
        P("layer", "tok", None),
        P("layer", "tok", None),
        P("layer", None, "tok", None),
        P("layer", None, "tok", None),
        P(),
    )
    out_specs = P("tok", "layer")

    def body(*args):
        return per_device(n_tok, n_layer, *args)

    return jax.shard_map(body, mesh=mesh, in_specs=in_specs, out_specs=out_specs, check_vma=False)
```
